32 devices in a mesh: groups: 2 (over x), seq: 16 (over z, y, core).
Axes of the slice: x: 2, y: 2, z: 4, core: 2. Of those that a mesh axis runs over, the one named last changes fastest.
Arguments:
- window_queries: bfloat16 [4096, 2048], P(('groups', 'seq')), parts along dimension 0, may hold values from -300 to 300
- window_kv: bfloat16 [4096, 512], P(('groups', 'seq')), parts along dimension 0, may hold values from -6 to 6
- stream: bfloat16 [4096, 2880], P(('groups', 'seq')), parts along dimension 0, may hold values from -6 to 6
- moe_gain: float32 [2880], replicated, may hold values from 0.25 to 1.75
- routes: int32 [4096, 4], P(('groups', 'seq')), parts along dimension 0, may hold values from 0 to 15, as said below
- route_gates: float32 [4096, 4], P(('groups', 'seq')), parts along dimension 0, may hold values from 0.1 to 0.6
- gate_proj: bfloat16 [2880, 23040], P(None, 'seq'), may hold values from -0.109375 to 0.109375
- up_proj: bfloat16 [2880, 23040], P(None, 'seq'), may hold values from -0.109375 to 0.109375
- down_proj: bfloat16 [23040, 2880], P('seq'), may hold values from -0.15625 to 0.15625
- attn_gain: float32 [2880], replicated, may hold values from 0.25 to 1.75
- kv_proj: bfloat16 [2880, 512], replicated, may hold values from -0.109375 to 0.109375
- tract_queries: bfloat16 [4096, 2048], P(('groups', 'seq')), parts along dimension 0, may hold values from -300 to 300
Outputs:
- attn_window: bfloat16 [4096, 2048], P(('groups', 'seq')), parts along dimension 0
- stream_next: bfloat16 [4096, 2880], P(('groups', 'seq')), parts along dimension 0
- attn_tract: bfloat16 [4096, 2048], P(('groups', 'seq')), parts along dimension 0
The draws below stay inside these ranges and needn't reach their ends.
There are 2 independent parts, one for each index of `groups`. The reference program is written for one: setup_inputs(seed, part) draws one part's arguments, and reference() takes and returns one part's arrays. A program takes and returns all parts, laid end to end along the dimension named above; an argument that names none is the same for every part. Nothing has to cross between parts.
Inputs may be any that keep to these rules, and one draw needn't show every extreme that they name: `routes`: in each device's block of 128 tokens every expert is named exactly 32 times; a token names 4 different experts.
All inputs are finite; a program needn't handle non-finite values.
Results may differ from the reference program's by a relative error of at most 0.025.
The reference program's roundings to bfloat16 on the way (of `attend`, `moe_input`, `hidden`, `block_out`, `attn_input` and `tract_kv`) count: a program that leaves them out, or rounds other values in their place, can miss the bound.
Values may be sent and summed in bfloat16 or wider, within the bound.
No kernel may reach another device: no remote copies, remote signals or barrier semaphores. Data moves between devices by JAX's collectives and lax.ppermute only.
A program may use at most 128 MiB of HBM per device.

```python
import jax
import jax.numpy as jnp
from jax import lax

D = 2880
HEADS = 32
KV_HEADS = 4
HEAD_DIM = 64
EXPERTS = 16
FF = 1440
TOP = 4
WINDOW = 128
STRETCH = 1024
TOK_DEV = 128
TOKENS = 2048
CAP = 32
SPLIT = 1
PIECE = 1440
N_SEQ = 16


def query_draw(key):
    values = jnp.clip(jax.random.normal(key, (TOKENS, HEADS * HEAD_DIM), jnp.float32), -6.0, 6.0)
    return values.astype(jnp.bfloat16)


def draw_window_queries(key, part):
    return query_draw(jax.random.fold_in(key, 11))


def draw_tract_queries(key, part):
    return query_draw(jax.random.fold_in(key, 23))


def route_block(key):
    group_size = EXPERTS // TOP
    labels = jax.random.permutation(jax.random.fold_in(key, 1), EXPERTS).astype(jnp.int32)
    row_index = jnp.arange(TOK_DEV, dtype=jnp.int32)
    col_index = jnp.arange(TOP, dtype=jnp.int32)
    base_table = labels[col_index[None, :] * group_size + row_index[:, None] // CAP]

    def column_order(index):
        return jax.random.permutation(jax.random.fold_in(key, 100 + index), TOK_DEV).astype(jnp.int32)
    orders = jax.vmap(column_order)(col_index)
    route_table = base_table[jnp.transpose(orders), col_index[None, :]]
    half_rows = TOK_DEV // 2
    upper_rows = route_table[:half_rows]
    lower_rows = route_table[half_rows:]
    coin_flip = jax.random.randint(jax.random.fold_in(key, 2), (half_rows,), 0, 2) == 1
    swap_ok = coin_flip & (upper_rows[:, 1] != lower_rows[:, 1]) & (upper_rows[:, 0] != lower_rows[:, 0])
    upper_first = jnp.where(swap_ok, lower_rows[:, 1], upper_rows[:, 0])
    lower_second = jnp.where(swap_ok, upper_rows[:, 0], lower_rows[:, 1])
    upper_rows = upper_rows.at[:, 0].set(upper_first)
    lower_rows = lower_rows.at[:, 1].set(lower_second)
    route_table = jnp.concatenate([upper_rows, lower_rows], 0)
    turn_by = jax.random.randint(jax.random.fold_in(key, 3), (TOK_DEV, 1), 0, TOP)
    route_table = jnp.take_along_axis(route_table, (col_index[None, :] + turn_by) % TOP, axis=1)
    return route_table.astype(jnp.int32)


def draw_routes(key, part):
    block_count = TOKENS // TOK_DEV
    base_key = jax.random.fold_in(key, 31)
    block_keys = jax.vmap(lambda index: jax.random.fold_in(base_key, index))(jnp.arange(block_count, dtype=jnp.int32))
    tables = jax.vmap(route_block)(block_keys)
    return tables.reshape(TOKENS, TOP).astype(jnp.int32)


def steps_of(key, extent, split, smallest, largest):
    factor_of, own = 1.0, jax.random.fold_in(key, 6)
    for position, shards_of in split:
        heights = jnp.exp(jax.random.uniform(jax.random.fold_in(own, position), (shards_of,), jnp.float32, smallest / len(split), largest / len(split)))
        factor_of = factor_of * jnp.repeat(heights, extent[position] // shards_of).reshape([-1 if axis == position else 1 for axis in range(len(extent))])
    return factor_of


def scatter_about(own_key, shape, spread, most, split=(), kind=jnp.bfloat16):
    loudness = steps_of(own_key, shape, split, -0.22, 0.18) if split else 1.0
    array = jax.random.normal(own_key, shape, jnp.float32) * spread * loudness
    return jnp.minimum(jnp.maximum(array, -most), most).astype(kind)


def setup_inputs(seed: int = 0, part: int = 0) -> dict:
    arg_keys = jax.random.split(jax.random.key(seed), 13)
    part_keys = jax.random.split(jax.random.fold_in(arg_keys[12], part), 13)
    return {
        "window_queries": draw_window_queries(jax.random.fold_in(jax.random.fold_in(arg_keys[12], part), 71), part),
        "window_kv": scatter_about(part_keys[1], (TOKENS, 2 * KV_HEADS * HEAD_DIM), 1.0, 6.0, ((0, 16),)),
        "stream": scatter_about(part_keys[2], (TOKENS, D), 1.0, 6.0, ((0, 16),)),
        "moe_gain": jnp.clip(1.0 + 0.15 * jax.random.normal(arg_keys[3], (D,), jnp.float32), 0.25, 1.75),
        "routes": draw_routes(jax.random.fold_in(jax.random.fold_in(arg_keys[12], part), 71), part),
        "route_gates": jnp.clip(0.1 + 0.5 * jax.random.uniform(part_keys[5], (TOKENS, TOP), jnp.float32) ** steps_of(part_keys[5], (TOKENS, TOP), ((0, 16),), -0.2, 0.2), 0.1, 0.6),
        "gate_proj": scatter_about(arg_keys[6], (D, EXPERTS * FF), D ** -0.5, 0.109375, ((1, 16),)),
        "up_proj": scatter_about(arg_keys[7], (D, EXPERTS * FF), D ** -0.5, 0.109375, ((1, 16),)),
        "down_proj": scatter_about(arg_keys[8], (EXPERTS * FF, D), FF ** -0.5, 0.15625, ((0, 16),)),
        "attn_gain": jnp.clip(1.0 + 0.15 * jax.random.normal(arg_keys[9], (D,), jnp.float32), 0.25, 1.75),
        "kv_proj": scatter_about(arg_keys[10], (D, 2 * KV_HEADS * HEAD_DIM), D ** -0.5, 0.109375),
        "tract_queries": draw_tract_queries(jax.random.fold_in(jax.random.fold_in(arg_keys[12], part), 71), part),
    }


def normed(values, gain):
    widened = values.astype(jnp.float32)
    second = lax.optimization_barrier(jnp.mean(widened * widened, axis=-1, keepdims=True))
    return (widened * lax.rsqrt(second + 1e-05) * gain).astype(jnp.bfloat16)

def attend(queries, keys, values, allowed):
    query_rows = queries.shape[0]
    key_rows = keys.shape[0]
    group_size = HEADS // KV_HEADS
    query_heads = queries.astype(jnp.float32).reshape(query_rows, KV_HEADS, group_size, HEAD_DIM)
    key_heads = keys.astype(jnp.float32).reshape(key_rows, KV_HEADS, HEAD_DIM)
    value_heads = values.astype(jnp.float32).reshape(key_rows, KV_HEADS, HEAD_DIM)
    scores = jnp.einsum('qkgd,skd->kgqs', query_heads, key_heads) * 0.125
    scores = jnp.where(allowed, scores, -1e+30)
    peak = lax.optimization_barrier(jnp.max(scores, axis=-1, keepdims=True))
    weights = jnp.exp(scores - peak)
    totals = lax.optimization_barrier(jnp.sum(weights, axis=-1))
    rounded = lax.optimization_barrier(weights.astype(jnp.bfloat16)).astype(jnp.float32)
    mixed = jnp.einsum('kgqs,skd->qkgd', rounded, value_heads)
    mixed = mixed / jnp.transpose(totals, (2, 0, 1))[..., None]
    return mixed.reshape(query_rows, HEADS * HEAD_DIM).astype(jnp.bfloat16)

def reference(window_queries, window_kv, stream, moe_gain, routes, route_gates, gate_proj, up_proj, down_proj, attn_gain, kv_proj, tract_queries):
    half_cols = KV_HEADS * HEAD_DIM
    query_block = min(512, TOKENS)
    padded = jnp.concatenate([jnp.zeros((WINDOW, 2 * half_cols), jnp.bfloat16), window_kv], 0)

    def window_block(block_index):
        offset = block_index * query_block
        queries = lax.dynamic_slice_in_dim(window_queries, offset, query_block, 0)
        nearby = lax.dynamic_slice_in_dim(padded, offset, query_block + WINDOW, 0)
        query_pos = offset + jnp.arange(query_block, dtype=jnp.int32)
        key_pos = offset - WINDOW + jnp.arange(query_block + WINDOW, dtype=jnp.int32)
        distance = query_pos[:, None] - key_pos[None, :]
        allowed = (distance >= 0) & (distance < WINDOW) & (key_pos[None, :] >= 0)
        return attend(queries, nearby[:, :half_cols], nearby[:, half_cols:], allowed)
    attn_window = lax.map(window_block, jnp.arange(TOKENS // query_block, dtype=jnp.int32)).reshape(TOKENS, HEADS * HEAD_DIM)
    moe_input = normed(stream, moe_gain)
    flat_routes = routes.reshape(N_SEQ, TOK_DEV * TOP)
    onehot = (flat_routes[:, :, None] == jnp.arange(EXPERTS, dtype=jnp.int32)[None, None, :]).astype(jnp.int32)
    slot_rank = lax.optimization_barrier(jnp.sum(onehot * (jnp.cumsum(onehot, axis=1) - 1), axis=2))
    device_rows = jnp.arange(N_SEQ, dtype=jnp.int32)[:, None]
    token_ids = device_rows * TOK_DEV + jnp.arange(TOK_DEV * TOP, dtype=jnp.int32)[None, :] // TOP
    slot_index = flat_routes * CAP + slot_rank
    slot_table = jnp.zeros((N_SEQ, EXPERTS * CAP), jnp.int32).at[device_rows, slot_index].set(token_ids)
    gathered = moe_input[slot_table].reshape(N_SEQ, EXPERTS, CAP, D)

    def expert_out(expert):
        expert_rows = lax.dynamic_index_in_dim(gathered, expert, 1, keepdims=False).reshape(N_SEQ * CAP, D)
        summed = jnp.zeros((N_SEQ * CAP, D), jnp.float32)
        for part_index in range(SPLIT):
            first_col = expert * FF + part_index * PIECE
            gate_cols = lax.dynamic_slice_in_dim(gate_proj, first_col, PIECE, 1)
            up_cols = lax.dynamic_slice_in_dim(up_proj, first_col, PIECE, 1)
            down_rows = lax.dynamic_slice_in_dim(down_proj, first_col, PIECE, 0)
            gate_vals = jnp.dot(expert_rows, gate_cols, preferred_element_type=jnp.float32)
            up_vals = jnp.dot(expert_rows, up_cols, preferred_element_type=jnp.float32)
            hidden = (jax.nn.silu(gate_vals) * up_vals).astype(jnp.bfloat16)
            block_out = jnp.dot(hidden, down_rows, preferred_element_type=jnp.float32).astype(jnp.bfloat16)
            summed = summed + block_out.astype(jnp.float32)
        return summed.reshape(N_SEQ, CAP, D)
    outputs = lax.map(expert_out, jnp.arange(EXPERTS, dtype=jnp.int32))
    flat_out = outputs.reshape(EXPERTS * N_SEQ * CAP, D)
    picked_index = ((flat_routes * N_SEQ + device_rows) * CAP + slot_rank).reshape(-1)
    picked = flat_out[picked_index].reshape(TOKENS, TOP, D)
    stream_next = (stream.astype(jnp.float32) + lax.optimization_barrier(jnp.sum(picked * route_gates[:, :, None], axis=1))).astype(jnp.bfloat16)
    attn_input = normed(stream_next, attn_gain)
    tract_kv = jnp.dot(attn_input, kv_proj, preferred_element_type=jnp.float32).astype(jnp.bfloat16)
    lead = STRETCH // 2
    padded_kv = jnp.concatenate([jnp.zeros((lead, 2 * half_cols), jnp.bfloat16), tract_kv], 0)

    def stretch_block(block_index):
        offset = block_index * STRETCH
        queries = lax.dynamic_slice_in_dim(tract_queries, offset, STRETCH, 0)
        context = lax.dynamic_slice_in_dim(padded_kv, offset, STRETCH + lead, 0)
        query_pos = offset + jnp.arange(STRETCH, dtype=jnp.int32)
        key_pos = offset - lead + jnp.arange(STRETCH + lead, dtype=jnp.int32)
        allowed = (key_pos[None, :] <= query_pos[:, None]) & (key_pos[None, :] >= 0) & ((key_pos[None, :] + lead) // STRETCH == (query_pos[:, None] + lead) // STRETCH)
        return attend(queries, context[:, :half_cols], context[:, half_cols:], allowed)
    attn_tract = lax.map(stretch_block, jnp.arange(TOKENS // STRETCH, dtype=jnp.int32)).reshape(TOKENS, HEADS * HEAD_DIM)
    return (attn_window, stream_next, attn_tract)
```

```python
import functools

import jax
import jax.numpy as jnp
from jax import lax
from jax.experimental import pallas as pl
from jax.experimental.pallas import tpu as pltpu
from jax.sharding import PartitionSpec as P

HEADS = 32
KV_HEADS = 4
HEAD_DIM = 64
EXPERTS = 16
TOP = 4
WINDOW = 128
STRETCH = 1024
EPS = 1e-05
MASKED = -1e30
NT = (((1,), (1,)), ((), ()))


def dot(a, b, dims=(((1,), (0,)), ((), ()))):
    return lax.dot_general(a, b, dims, preferred_element_type=jnp.float32)


def transposed(block):
    rows = block.shape[0]
    edges = list(range(0, rows, 128)) + [rows]
    parts = [block[a:b, :].T for a, b in zip(edges[:-1], edges[1:])]
    return jnp.concatenate(parts, axis=1)


def slots(routes, capacity):
    tokens = routes.shape[1]
    expert = lax.broadcasted_iota(jnp.int32, (EXPERTS, tokens), 0)
    named = jnp.zeros((EXPERTS, tokens), jnp.float32)
    for k in range(TOP):
        named = named + (routes[k : k + 1, :] == expert).astype(jnp.float32)
    before = lax.broadcasted_iota(jnp.int32, (tokens, tokens), 0)
    after = lax.broadcasted_iota(jnp.int32, (tokens, tokens), 1)
    ahead = (before < after).astype(jnp.bfloat16)
    rank = dot(named.astype(jnp.bfloat16), ahead).astype(jnp.int32)
    rank = jnp.where(named > 0.5, rank, -1)
    place = lax.broadcasted_iota(jnp.int32, (EXPERTS, capacity, tokens), 1)
    return (rank[:, None, :] == place).astype(jnp.float32)


def prep_kernel(routes_ref, stream_ref, gain_ref, out_ref):
    capacity = out_ref.shape[1]
    stream = stream_ref[...].astype(jnp.float32)
    second = jnp.sum(stream * stream, axis=0, keepdims=True) / stream.shape[0]
    scaled = stream * lax.rsqrt(second + EPS)
    tokens = (transposed(scaled) * gain_ref[...]).astype(jnp.bfloat16)
    chosen = slots(routes_ref[...], capacity)
    chosen = chosen.reshape(EXPERTS * capacity, -1).astype(jnp.bfloat16)
    rows = dot(chosen, tokens).astype(jnp.bfloat16)
    out_ref[...] = rows.reshape(out_ref.shape)


def prep(routes, stream, gain):
    rows, width = stream.shape
    capacity = rows * TOP // EXPERTS
    return pl.pallas_call(
        prep_kernel,
        out_shape=jax.ShapeDtypeStruct((EXPERTS, capacity, width), jnp.bfloat16),
        cost_estimate=pl.CostEstimate(
            flops=2 * rows * TOP * rows * width, bytes_accessed=12 * rows * width, transcendentals=0
        ),
        name="prep",
    )(routes.T, stream.T, gain.reshape(1, -1))


def experts_kernel(x_ref, gate_ref, up_ref, down_ref, out_ref, acc_ref):
    step = pl.program_id(1)
    rows = x_ref[...]
    gate = dot(rows, gate_ref[...], NT)
    up = dot(rows, up_ref[...], NT)
    hidden = (jax.nn.silu(gate) * up).astype(jnp.bfloat16)
    part = dot(hidden, down_ref[...])

    @pl.when(step == 0)
    def _():
        acc_ref[...] = part

    @pl.when(step > 0)
    def _():
        acc_ref[...] += part

    @pl.when(step == pl.num_programs(1) - 1)
    def _():
        out_ref[...] = acc_ref[...].astype(jnp.bfloat16)


def tile_of(extent, most, unit):
    for size in range(min(extent, most), 0, -1):
        if extent % size == 0 and (size % unit == 0 or size == extent):
            return size
    return extent


def experts(rows, gate_proj, up_proj, down_proj):
    count, width = rows.shape
    hidden = down_proj.shape[0]
    tile = tile_of(hidden, 480, 16)
    block = tile_of(count, 512, 16)
    return pl.pallas_call(
        experts_kernel,
        grid=(count // block, hidden // tile),
        in_specs=[
            pl.BlockSpec((block, width), lambda i, j: (i, 0)),
            pl.BlockSpec((tile, width), lambda i, j: (j, 0)),
            pl.BlockSpec((tile, width), lambda i, j: (j, 0)),
            pl.BlockSpec((tile, width), lambda i, j: (j, 0)),
        ],
        out_specs=pl.BlockSpec((block, width), lambda i, j: (i, 0)),
        out_shape=jax.ShapeDtypeStruct((count, width), jnp.bfloat16),
        scratch_shapes=[pltpu.VMEM((block, width), jnp.float32)],
        cost_estimate=pl.CostEstimate(
            flops=6 * count * width * hidden,
            bytes_accessed=6 * width * hidden + 4 * count * width,
            transcendentals=count * hidden,
        ),
        name="experts",
    )(rows, gate_proj.T, up_proj.T, down_proj)


def combine_kernel(
    routes_ref, gates_ref, returned_ref, stream_ref, gain_ref, proj_ref, next_ref, kv_ref
):
    splits, capacity = returned_ref.shape[1:3]
    width = returned_ref.shape[3]
    routes = routes_ref[...]
    tokens = routes.shape[1]
    expert = lax.broadcasted_iota(jnp.int32, (EXPERTS, tokens), 0)
    gate = jnp.zeros((EXPERTS, tokens), jnp.float32)
    for k in range(TOP):
        gate = gate + jnp.where(routes[k : k + 1, :] == expert, gates_ref[k : k + 1, :], 0.0)
    chosen = slots(routes, capacity) * gate[:, None, :]
    if splits > 1:
        chosen = jnp.broadcast_to(
            chosen[:, None], (EXPERTS, splits, capacity, tokens)
        )
    mix = transposed(chosen.reshape(EXPERTS * splits * capacity, tokens))
    high = mix.astype(jnp.bfloat16)
    rest = mix - high.astype(jnp.float32)
    middle = rest.astype(jnp.bfloat16)
    low = (rest - middle.astype(jnp.float32)).astype(jnp.bfloat16)
    parts = jnp.concatenate([high, middle, low], axis=0)
    summed = dot(parts, returned_ref[...].reshape(-1, width))
    summed = summed[:tokens] + (summed[tokens : 2 * tokens] + summed[2 * tokens :])
    stream = transposed(stream_ref[...].astype(jnp.float32))
    following = (stream + summed).astype(jnp.bfloat16)
    widened = following.astype(jnp.float32)
    for a in range(0, width, 128):
        b = min(a + 128, width)
        next_ref[a:b, :] = widened[:, a:b].T.astype(jnp.bfloat16)
    second = jnp.sum(widened * widened, axis=1, keepdims=True) / width
    attn_input = (widened * lax.rsqrt(second + EPS) * gain_ref[...]).astype(jnp.bfloat16)
    kv_ref[...] = dot(attn_input, proj_ref[...]).astype(jnp.bfloat16)


def combine(routes, gates, returned, stream, gain, kv_proj):
    rows, width = stream.shape
    following, kv = pl.pallas_call(
        combine_kernel,
        out_shape=(
            jax.ShapeDtypeStruct((width, rows), jnp.bfloat16),
            jax.ShapeDtypeStruct((rows, kv_proj.shape[1]), jnp.bfloat16),
        ),
        cost_estimate=pl.CostEstimate(
            flops=6 * rows * TOP * rows * width,
            bytes_accessed=2 * returned.size + 4 * rows * width + 2 * kv_proj.size,
            transcendentals=0,
        ),
        name="combine",
    )(routes.T, gates.T, returned, stream.T, gain.reshape(1, -1), kv_proj)
    return following.T, kv


def spread(block, left):
    empty = jnp.zeros_like(block)
    return jnp.concatenate([block, empty] if left else [empty, block], axis=1)


def attend_kernel(mask_fn, *refs):
    scalar_ref, query_ref, own_ref = refs[:3]
    other_refs, out_ref = refs[3:-1], refs[-1]
    rows = query_ref.shape[0]
    half = own_ref.shape[1] // 2
    pairs = query_ref.shape[1] // (2 * HEAD_DIM)
    per_kv = pairs // KV_HEADS
    shared = sum(ref.shape[0] for ref in other_refs)
    own_mask, other_mask = mask_fn(scalar_ref, rows, shared)
    own_mask = jnp.concatenate([own_mask] * per_kv, axis=0)
    if other_mask.shape[0] > 1:
        other_mask = jnp.concatenate([other_mask] * per_kv, axis=0)
    lane = lax.broadcasted_iota(jnp.int32, (per_kv * rows, 2 * HEAD_DIM), 1)
    for g in range(KV_HEADS):
        cols = slice(g * HEAD_DIM, (g + 1) * HEAD_DIM)
        vcols = slice(half + g * HEAD_DIM, half + (g + 1) * HEAD_DIM)
        queries = jnp.concatenate(
            [
                query_ref[:, (g * per_kv + p) * 2 * HEAD_DIM : (g * per_kv + p + 1) * 2 * HEAD_DIM]
                for p in range(per_kv)
            ],
            axis=0,
        )
        own_keys = own_ref[:, cols] * jnp.bfloat16(0.125)
        other_keys = jnp.concatenate([ref[:, cols] for ref in other_refs], axis=0)
        other_keys = other_keys * jnp.bfloat16(0.125)
        own_values = own_ref[:, vcols]
        other_values = jnp.concatenate([ref[:, vcols] for ref in other_refs], axis=0)
        mixed, totals = [], []
        for left in (True, False):
            own = dot(queries, spread(own_keys, left), NT)
            other = dot(queries, spread(other_keys, left), NT)
            own = jnp.where(own_mask, own, MASKED)
            other = jnp.where(other_mask, other, MASKED)
            peak = jnp.maximum(
                jnp.max(own, axis=1, keepdims=True), jnp.max(other, axis=1, keepdims=True)
            )
            own = jnp.exp(own - peak)
            other = jnp.exp(other - peak)
            totals.append(
                jnp.sum(own, axis=1, keepdims=True) + jnp.sum(other, axis=1, keepdims=True)
            )
            mixed.append(
                dot(own.astype(jnp.bfloat16), spread(own_values, left))
                + dot(other.astype(jnp.bfloat16), spread(other_values, left))
            )
        total = jnp.where(lane < HEAD_DIM, totals[0], totals[1])
        result = ((mixed[0] + mixed[1]) / total).astype(jnp.bfloat16)
        for p in range(per_kv):
            at = (g * per_kv + p) * 2 * HEAD_DIM
            out_ref[:, at : at + 2 * HEAD_DIM] = result[p * rows : (p + 1) * rows]


def attend(mask_fn, scalar, queries, own, others, name):
    rows, width = queries.shape
    keys = rows + sum(other.shape[0] for other in others)
    vmem = pl.BlockSpec(memory_space=pltpu.VMEM)
    return pl.pallas_call(
        functools.partial(attend_kernel, mask_fn),
        in_specs=[pl.BlockSpec(memory_space=pltpu.SMEM)] + [vmem] * (2 + len(others)),
        out_specs=vmem,
        out_shape=jax.ShapeDtypeStruct((rows, width), jnp.bfloat16),
        cost_estimate=pl.CostEstimate(
            flops=8 * rows * width * keys,
            bytes_accessed=4 * rows * width + 4 * keys * own.shape[1],
            transcendentals=rows * HEADS * keys,
        ),
        name=name,
    )(scalar, queries, own, *others)


def window_masks(scalar_ref, rows, shared):
    device = scalar_ref[0]
    token = lax.broadcasted_iota(jnp.int32, (rows, rows), 0)
    key = lax.broadcasted_iota(jnp.int32, (rows, rows), 1)
    own = (key <= token) & (token - key < WINDOW)
    token = lax.broadcasted_iota(jnp.int32, (rows, shared), 0)
    key = lax.broadcasted_iota(jnp.int32, (rows, shared), 1) - shared
    return own, (token - key < WINDOW) & (key + device * rows >= 0)


def tract_masks(scalar_ref, rows, shared):
    token = lax.broadcasted_iota(jnp.int32, (rows, rows), 0)
    key = lax.broadcasted_iota(jnp.int32, (rows, rows), 1)
    block = lax.broadcasted_iota(jnp.int32, (1, shared), 1) // rows
    valid = jnp.zeros((1, shared), jnp.int32)
    for b in range(shared // rows):
        valid = jnp.where(block == b, scalar_ref[b], valid)
    return key <= token, valid > 0


def exchange(own, device, devices, per_half):
    everyone = range(devices)
    odd = lambda i: (i // per_half) % 2 == 1
    route = [(i, i + per_half) for i in everyone if odd(i) and i + per_half < devices]
    before = lax.ppermute(own, "seq", route)
    held, sources = [before], [("before", 0)]
    group = (device // per_half) % 2
    has_before = ((group == 0) & (device >= per_half)).astype(jnp.int32)
    parts = [(own, before)]
    pack = jnp.concatenate([own, before], axis=0)
    others = [before]
    flags = [has_before]
    masks = [0]
    step = per_half // 2
    while step:
        came = lax.ppermute(pack, "seq", [(i, i ^ step) for i in everyone])
        others.append(came)
        for m in masks:
            flags.append(((device ^ (m ^ step)) < device).astype(jnp.int32))
            flags.append(has_before)
        masks = masks + [m ^ step for m in masks]
        pack = jnp.concatenate([pack, came], axis=0)
        step //= 2
    return others, jnp.stack(flags)


def on_device(
    window_queries,
    window_kv,
    stream,
    moe_gain,
    routes,
    route_gates,
    gate_proj,
    up_proj,
    down_proj,
    attn_gain,
    kv_proj,
    tract_queries,
):
    rows_here, model_width = stream.shape
    device = lax.axis_index("seq")
    devices = lax.axis_size("seq")
    capacity = rows_here * TOP // EXPERTS
    split_count = devices // EXPERTS
    rim = lax.ppermute(window_kv, "seq", [(i - 1, i) for i in range(1, devices)])
    outgoing = prep(routes, stream, moe_gain)
    copies = jnp.repeat(outgoing, split_count, axis=0) if split_count > 1 else outgoing
    arrived = lax.all_to_all(copies, "seq", split_axis=0, concat_axis=0, tiled=True)
    block_out = experts(arrived.reshape(-1, model_width), gate_proj, up_proj, down_proj)
    returned = lax.all_to_all(
        block_out.reshape(arrived.shape), "seq", split_axis=0, concat_axis=0, tiled=True
    )
    attn_window = attend(
        window_masks, device.reshape(1).astype(jnp.int32), window_queries, window_kv, [rim], "window"
    )
    returned = returned.reshape(EXPERTS, split_count, capacity, model_width)
    stream_next, tract_kv = combine(routes, route_gates, returned, stream, attn_gain, kv_proj)
    per_half = STRETCH // 2 // rows_here
    others, flags = exchange(tract_kv, device, devices, per_half)
    attn_tract = attend(tract_masks, flags, tract_queries, tract_kv, others, "tract")
    return (attn_window, stream_next, attn_tract)


def solution(mesh):
    return jax.shard_map(
        on_device,
        mesh=mesh,
        in_specs=(
            P(("groups", "seq"), None),
            P(("groups", "seq"), None),
            P(("groups", "seq"), None),
            P(),
            P(("groups", "seq"), None),
            P(("groups", "seq"), None),
            P(None, "seq"),
            P(None, "seq"),
            P("seq", None),
            P(),
            P(),
            P(("groups", "seq"), None),
        ),
        out_specs=(
            P(("groups", "seq"), None),
            P(("groups", "seq"), None),
            P(("groups", "seq"), None),
        ),
        check_vma=False,
    )
```
